32 devices in a mesh: dp: 16 (over z, y, x), mp: 2 (over core).
Axes of the slice: x: 2, y: 2, z: 4, core: 2. Of those that a mesh axis runs over, the one named last changes fastest.
Arguments:
- tokens: bfloat16 [16384, 768], P('dp'), may hold values from -6 to 6
- cotangent: bfloat16 [16384, 768], P('dp'), may hold values from -6 to 6
- lengths: int32 [16, 16], P('dp'), may hold values from 0 to 900, as said below
- ln1_gain: float32 [768], replicated, may hold values from 0.5 to 1.5
- ln1_bias: float32 [768], replicated, may hold values from -1.5 to 1.5
- qkv_weight: bfloat16 [768, 3, 768], P(None, None, 'mp'), may hold values from -0.21875 to 0.21875
- qv_bias: float32 [2, 768], P(None, 'mp'), may hold values from -2.5 to 2.5
- out_weight: bfloat16 [768, 768], P('mp'), may hold values from -0.875 to 0.875
- out_bias: float32 [768], replicated, may hold values from -1.5 to 1.5
- ln2_gain: float32 [768], replicated, may hold values from 0.5 to 1.5
- ln2_bias: float32 [768], replicated, may hold values from -1.5 to 1.5
- up_weight: bfloat16 [768, 3072], P(None, 'mp'), may hold values from -0.21875 to 0.21875
- up_bias: float32 [3072], P('mp'), may hold values from -2.5 to 2.5
- down_weight: bfloat16 [3072, 768], P('mp'), may hold values from -0.109375 to 0.109375
- down_bias: float32 [768], replicated, may hold values from -1.5 to 1.5
Outputs:
- output: bfloat16 [16384, 768], P('dp')
- tokens_grad: float32 [16384, 768], P('dp')
- ln1_gain_grad: float32 [768], replicated
- ln1_bias_grad: float32 [768], replicated
- qkv_weight_grad: float32 [768, 3, 768], P('dp', None, 'mp')
- qv_bias_grad: float32 [2, 768], P(None, 'mp')
- out_weight_grad: float32 [768, 768], P('mp', 'dp')
- out_bias_grad: float32 [768], replicated
- ln2_gain_grad: float32 [768], replicated
- ln2_bias_grad: float32 [768], replicated
- up_weight_grad: float32 [768, 3072], P('dp', 'mp')
- up_bias_grad: float32 [3072], P('mp')
- down_weight_grad: float32 [3072, 768], P('mp', 'dp')
- down_bias_grad: float32 [768], replicated
The draws below stay inside these ranges and needn't reach their ends.
Inputs may be any that keep to these rules, and one draw needn't show every extreme that they name: Each length is 0 or the square of one of 30, 15, 10, 6, 5. The lengths of one index of dp sum to at most 1024; its images lie one after another from its row 0 in slot order, and its remaining rows are padding.
All inputs are finite; a program needn't handle non-finite values.
Results may differ from the reference program's by a relative error of at most 0.012.
The reference program's roundings to bfloat16 on the way count: a program that leaves them out, or rounds other values in their place, can miss the bound.
Values may be sent and summed in bfloat16 or wider, within the bound.
No kernel may reach another device: no remote copies, remote signals or barrier semaphores. Data moves between devices by JAX's collectives and lax.ppermute only.
A program may use at most 192 MiB of HBM per device.

```python
import jax
import jax.numpy as jnp
from jax import lax

D = 768
HEADS = 12
HEAD_DIM = 64
FF = 3072
CAP = 1024
IMG_DEV = 16
GRID = 30
ROWS = 16384
N_DP = 16


def draw_lengths(key, part):
    key_heavy, key_pick, key_rank = jax.random.split(key, 3)
    coarse_sizes = jnp.array([(GRID // 2) ** 2, (GRID // 3) ** 2, (GRID // 5) ** 2, (GRID // 6) ** 2], jnp.int32)
    is_heavy = jax.random.randint(key_heavy, (N_DP,), 0, 8) == 0
    chosen = jax.random.randint(key_rank, (), 0, N_DP)
    is_heavy = jnp.logical_or(is_heavy, jnp.arange(N_DP) == chosen)
    drawn = jax.random.randint(key_pick, (N_DP, IMG_DEV), 0, 4)
    wanted = coarse_sizes[drawn]
    wanted = wanted.at[:, 0].set(jnp.where(is_heavy, GRID * GRID, wanted[:, 0]))
    running = jnp.zeros((N_DP,), jnp.int32)
    columns = []
    for slot_index in range(IMG_DEV):
        fitting = running + wanted[:, slot_index] <= CAP
        accepted = jnp.where(fitting, wanted[:, slot_index], 0).astype(jnp.int32)
        running = running + accepted
        columns.append(accepted)
    return jnp.stack(columns, axis=1).astype(jnp.int32)


def strengthened(values, stream_key, source, target, blocks, factor):
    owner, partner = [(jnp.arange(values.shape[axis_at]) // (values.shape[axis_at] // blocks)).reshape([-1 if axis == axis_at else 1 for axis in range(values.ndim)]) for axis_at in (source, target)]
    chosen = jax.random.permutation(stream_key, blocks)[partner]
    strong = (owner == chosen) | (owner == (partner + blocks // 2) % blocks)
    return jnp.where(strong, factor * values, values)


def levels(stream_key, extent, cuts, least, high):
    def one(dim, blocks):
        heights = jax.random.uniform(jax.random.fold_in(jax.random.fold_in(stream_key, 6), dim), (blocks,), jnp.float32, least / len(cuts), high / len(cuts))
        return jnp.repeat(jnp.exp(heights), extent[dim] // blocks).reshape((-1,) + (1,) * (len(extent) - dim - 1))

    level = one(*cuts[0])
    for cut in cuts[1:]:
        level = level * one(*cut)
    return level


def normal_values(key, extent, scale, bound, pieces=(), held_as=jnp.bfloat16):
    level = levels(key, extent, pieces, -0.22, 0.18) if pieces else 1.0
    values = jax.random.normal(key, extent, jnp.float32) * scale * level
    return jnp.minimum(jnp.maximum(values, -bound), bound).astype(held_as)


def gaussian_with(own_key, shape, spread, most, cuts, heavy, held_as=jnp.bfloat16):
    values = spread * jax.random.normal(own_key, shape, jnp.float32)
    if cuts:
        values = values * levels(own_key, shape, cuts, -0.22, 0.18)
    return jnp.clip(strengthened(values, jax.random.fold_in(own_key, 3), *heavy), -most, most).astype(held_as)


def setup_inputs(seed: int = 0) -> dict:
    key_list = jax.random.split(jax.random.key(seed), 16)
    return {
        "tokens": normal_values(key_list[0], (ROWS, D), 1.0, 6.0, ((0, 16),)),
        "cotangent": gaussian_with(key_list[1], (ROWS, D), 1.0, 6.0, ((0, 16),), (0, 1, 16, 2.0)),
        "lengths": draw_lengths(jax.random.fold_in(key_list[15], 71), 0),
        "ln1_gain": jnp.clip(1.0 + 0.1 * jax.random.normal(key_list[3], (D,), jnp.float32), 0.5, 1.5),
        "ln1_bias": normal_values(key_list[4], (D,), 0.3, 1.5, (), jnp.float32),
        "qkv_weight": normal_values(key_list[5], (D, 3, D), D ** -0.5, 0.21875, ((2, 2),)),
        "qv_bias": normal_values(key_list[6], (2, D), 0.5, 2.5, ((1, 2),), jnp.float32),
        "out_weight": normal_values(key_list[7], (D, D), (D // 16) ** -0.5, 0.875, ((0, 2),)),
        "out_bias": normal_values(key_list[8], (D,), 0.3, 1.5, (), jnp.float32),
        "ln2_gain": jnp.clip(1.0 + 0.1 * jax.random.normal(key_list[9], (D,), jnp.float32), 0.5, 1.5),
        "ln2_bias": normal_values(key_list[10], (D,), 0.3, 1.5, (), jnp.float32),
        "up_weight": normal_values(key_list[11], (D, FF), D ** -0.5, 0.21875, ((1, 2),)),
        "up_bias": normal_values(key_list[12], (FF,), 0.5, 2.5, ((0, 2),), jnp.float32),
        "down_weight": normal_values(key_list[13], (FF, D), FF ** -0.5, 0.109375, ((0, 2),)),
        "down_bias": normal_values(key_list[14], (D,), 0.3, 1.5, (), jnp.float32),
    }


EPSILON = 1e-06
HIGHEST_PRECISION = lax.Precision.HIGHEST

@jax.custom_vjp
def low(v):
    return lax.optimization_barrier(v.astype(jnp.bfloat16)).astype(jnp.float32)

@jax.custom_vjp
def low_back(v):
    return v

def low_keep(v):
    return (low(v), None)

def low_pass(kept, grad):
    return (grad,)

def back_keep(v):
    return (v, None)

def back_low(kept, grad):
    return (low(grad),)
low.defvjp(low_keep, low_pass)
low_back.defvjp(back_keep, back_low)

def layer_norm(values, gain, shift):
    centered = values - lax.optimization_barrier(jnp.mean(values, axis=-1, keepdims=True))
    variance = lax.optimization_barrier(jnp.mean(centered * centered, axis=-1, keepdims=True))
    return centered * lax.rsqrt(variance + EPSILON) * gain + shift

def device_rows(params, row_pair):
    tokens_dev, image_ids = row_pair
    ln1_gain, ln1_bias, qkv_weight, qv_bias, out_weight, out_bias, ln2_gain, ln2_bias, up_weight, up_bias, down_weight, down_bias = params
    row_count = tokens_dev.shape[0]
    hidden_one = low(layer_norm(tokens_dev, ln1_gain, ln1_bias))
    queries = jnp.dot(hidden_one, qkv_weight[:, 0, :], precision=HIGHEST_PRECISION) + qv_bias[0]
    keys_all = jnp.dot(hidden_one, qkv_weight[:, 1, :], precision=HIGHEST_PRECISION)
    values_all = jnp.dot(hidden_one, qkv_weight[:, 2, :], precision=HIGHEST_PRECISION) + qv_bias[1]
    queries = low(low_back(queries)).reshape(row_count, HEADS, HEAD_DIM)
    keys_all = low(low_back(keys_all)).reshape(row_count, HEADS, HEAD_DIM)
    values_all = low(low_back(values_all)).reshape(row_count, HEADS, HEAD_DIM)
    scores = jnp.einsum('qhd,khd->hqk', queries, keys_all, precision=HIGHEST_PRECISION) * HEAD_DIM ** (-0.5)
    scores = low_back(scores)
    same_image = image_ids[:, None] == image_ids[None, :]
    scores = jnp.where(same_image[None], scores, -1e+30)
    largest = lax.optimization_barrier(jnp.max(scores, axis=-1, keepdims=True))
    exponent = jnp.exp(scores - largest)
    probs = exponent / lax.optimization_barrier(jnp.sum(exponent, axis=-1, keepdims=True))
    mixed = jnp.einsum('hqk,khd->qhd', low(probs), values_all, precision=HIGHEST_PRECISION)
    mixed = low(low_back(mixed)).reshape(row_count, HEADS * HEAD_DIM)
    attended = jnp.dot(mixed, out_weight, precision=HIGHEST_PRECISION) + out_bias
    after_attn = tokens_dev + low_back(attended)
    hidden_two = low(layer_norm(after_attn, ln2_gain, ln2_bias))
    hidden_pre = low_back(jnp.dot(hidden_two, up_weight, precision=HIGHEST_PRECISION) + up_bias)
    activated = low(jax.nn.gelu(hidden_pre, approximate=True))
    branch = low_back(jnp.dot(activated, down_weight, precision=HIGHEST_PRECISION) + down_bias)
    return after_attn + branch

def reference(tokens, cotangent, lengths, ln1_gain, ln1_bias, qkv_weight, qv_bias, out_weight, out_bias, ln2_gain, ln2_bias, up_weight, up_bias, down_weight, down_bias):
    ends = jnp.cumsum(lengths, axis=1).astype(jnp.int32)
    positions = jnp.arange(CAP).astype(jnp.int32)
    image_ids = lax.optimization_barrier(jnp.sum((ends[:, None, :] <= positions[None, :, None]).astype(jnp.int32), axis=2)).astype(jnp.int32)
    valid = (image_ids < IMG_DEV).astype(jnp.float32).reshape(N_DP * CAP)
    params = tuple((item.astype(jnp.float32) for item in (ln1_gain, ln1_bias, qkv_weight, qv_bias, out_weight, out_bias, ln2_gain, ln2_bias, up_weight, up_bias, down_weight, down_bias)))
    checked = jax.checkpoint(device_rows)

    def forward(inputs_all, weights_all):
        stacked = inputs_all.reshape(N_DP, CAP, D)
        results = lax.map(lambda row_pair: checked(weights_all, row_pair), (stacked, image_ids))
        return results.reshape(N_DP * CAP, D)
    result, pullback = jax.vjp(forward, tokens.astype(jnp.float32), params)
    grad_out = cotangent.astype(jnp.float32) * valid[:, None]
    grad_in, grads = pullback(grad_out)
    return (result.astype(jnp.bfloat16), grad_in, grads[0], grads[1], grads[2], grads[3], grads[4], grads[5], grads[6], grads[7], grads[8], grads[9], grads[10], grads[11])
```

```python
import functools

import jax
import jax.numpy as jnp
from jax import lax
from jax.experimental import pallas as pl
from jax.experimental.pallas import tpu as pltpu
from jax.sharding import PartitionSpec as P

HEAD_DIM = 64
EPSILON = 1e-06
F32 = jnp.float32
BF16 = jnp.bfloat16
NT = (((1,), (1,)), ((), ()))


def normalize(values):
    centered = values - jnp.mean(values, axis=-1, keepdims=True)
    variance = jnp.mean(centered * centered, axis=-1, keepdims=True)
    inverse = lax.rsqrt(variance + EPSILON)
    return (centered * inverse, inverse)


def norm_back(grad_out, normed, inverse, gain):
    scaled = grad_out * gain
    return inverse * (
        scaled
        - jnp.mean(scaled, axis=-1, keepdims=True)
        - normed * jnp.mean(scaled * normed, axis=-1, keepdims=True)
    )


def gelu_back(hidden_pre, grad_act):
    unused, pullback = jax.vjp(lambda value: jax.nn.gelu(value, approximate=True), hidden_pre)
    return pullback(grad_act)[0]


def own_half(shape, half):
    lane = lax.broadcasted_iota(jnp.int32, shape, 1)
    return (lane < HEAD_DIM) if half == 0 else (lane >= HEAD_DIM)


def attention_forward_kernel(idk_ref, idq_ref, q_ref, k_ref, v_ref, pt_ref, o_ref, bias_ref):
    @pl.when(pl.program_id(1) == 0)
    def _():
        bias_ref[...] = jnp.where(idk_ref[...] == idq_ref[...], 0.0, -1e30)

    q = q_ref[...]
    k = k_ref[...]
    vt = v_ref[...].T
    outs = []
    for half in range(2):
        qm = jnp.where(own_half(q.shape, half), q, jnp.zeros_like(q))
        st = lax.dot_general(k, qm, NT, preferred_element_type=F32) + bias_ref[...]
        largest = jnp.max(st, axis=0, keepdims=True)
        exponent = jnp.exp(st - largest)
        total = jnp.sum(exponent, axis=0, keepdims=True)
        pt = (exponent * (1.0 / total)).astype(BF16)
        pt_ref[half] = pt
        outs.append(
            jnp.dot(vt[half * HEAD_DIM : (half + 1) * HEAD_DIM], pt, preferred_element_type=F32)
        )
    o_ref[...] = jnp.concatenate(outs, axis=0).T.astype(BF16)


def attention_forward(queries, keys, values, image_ids, block):
    rows, local = queries.shape
    pairs = local // (2 * HEAD_DIM)
    lanes = 2 * HEAD_DIM
    return pl.pallas_call(
        attention_forward_kernel,
        grid=(rows // block, pairs),
        in_specs=[
            pl.BlockSpec((rows, 1), lambda i, p: (0, 0)),
            pl.BlockSpec((1, block), lambda i, p: (0, i)),
            pl.BlockSpec((block, lanes), lambda i, p: (i, p)),
            pl.BlockSpec((rows, lanes), lambda i, p: (0, p)),
            pl.BlockSpec((rows, lanes), lambda i, p: (0, p)),
        ],
        out_specs=[
            pl.BlockSpec((2, rows, block), lambda i, p: (p, 0, i)),
            pl.BlockSpec((block, lanes), lambda i, p: (i, p)),
        ],
        out_shape=[
            jax.ShapeDtypeStruct((2 * pairs, rows, rows), BF16),
            jax.ShapeDtypeStruct((rows, local), BF16),
        ],
        scratch_shapes=[pltpu.VMEM((rows, block), F32)],
        cost_estimate=pl.CostEstimate(
            flops=16 * rows * rows * local, bytes_accessed=4 * pairs * rows * rows, transcendentals=0
        ),
        name="attention_forward",
    )(image_ids[:, None], image_ids[None, :], queries, keys, values)


def attention_backward_kernel(q_ref, k_ref, v_ref, do_ref, pt_ref, g_ref, dk_ref, dv_ref):
    pair, step = pl.program_id(0), pl.program_id(1)
    steps = pl.num_programs(1)
    block, lanes = q_ref.shape
    local = g_ref.shape[1] // 3
    q = q_ref[...]
    do = do_ref[...]
    k = k_ref[...]
    v = v_ref[...]
    kt = k.T
    dqs = []
    dk = None
    dv = None
    for half in range(2):
        mine = own_half(q.shape, half)
        qm = jnp.where(mine, q, jnp.zeros_like(q))
        dom = jnp.where(mine, do, jnp.zeros_like(do))
        pt = pt_ref[half]
        dpt = lax.dot_general(v, dom, NT, preferred_element_type=F32)
        ptf = pt.astype(F32)
        centre = jnp.sum(ptf * dpt, axis=0, keepdims=True)
        dst = (ptf * (dpt - centre)).astype(BF16)
        dv_half = jnp.dot(pt, dom, preferred_element_type=F32)
        dk_half = jnp.dot(dst, qm, preferred_element_type=F32)
        dv = dv_half if dv is None else dv + dv_half
        dk = dk_half if dk is None else dk + dk_half
        dqs.append(
            jnp.dot(kt[half * HEAD_DIM : (half + 1) * HEAD_DIM], dst, preferred_element_type=F32)
        )
    column = pl.multiple_of(pair * lanes, lanes)
    dq = jnp.concatenate(dqs, axis=0).T * (HEAD_DIM**-0.5)
    g_ref[pl.ds(pl.multiple_of(step * block, block), block), pl.ds(column, lanes)] = dq.astype(BF16)

    @pl.when(step == 0)
    def _():
        dk_ref[...] = dk
        dv_ref[...] = dv

    @pl.when(step > 0)
    def _():
        dk_ref[...] += dk
        dv_ref[...] += dv

    @pl.when(step == steps - 1)
    def _():
        g_ref[:, pl.ds(pl.multiple_of(local + column, lanes), lanes)] = dk_ref[...].astype(BF16)
        g_ref[:, pl.ds(pl.multiple_of(2 * local + column, lanes), lanes)] = dv_ref[...].astype(BF16)


def attention_backward(queries, keys, values, grad_mixed, probs, block):
    rows, local = queries.shape
    pairs = local // (2 * HEAD_DIM)
    lanes = 2 * HEAD_DIM
    return pl.pallas_call(
        attention_backward_kernel,
        grid=(pairs, rows // block),
        in_specs=[
            pl.BlockSpec((block, lanes), lambda p, i: (i, p)),
            pl.BlockSpec((rows, lanes), lambda p, i: (0, p)),
            pl.BlockSpec((rows, lanes), lambda p, i: (0, p)),
            pl.BlockSpec((block, lanes), lambda p, i: (i, p)),
            pl.BlockSpec((2, rows, block), lambda p, i: (p, 0, i)),
        ],
        out_specs=pl.BlockSpec((rows, 3 * local), lambda p, i: (0, 0)),
        out_shape=jax.ShapeDtypeStruct((rows, 3 * local), BF16),
        scratch_shapes=[pltpu.VMEM((rows, lanes), F32), pltpu.VMEM((rows, lanes), F32)],
        cost_estimate=pl.CostEstimate(
            flops=32 * rows * rows * local, bytes_accessed=4 * pairs * rows * rows, transcendentals=0
        ),
        name="attention_backward",
    )(queries, keys, values, grad_mixed, probs)


def swap_cores(part, cores):
    low = part.astype(BF16)
    total = low.astype(F32)
    for shift in range(1, cores):
        other = lax.ppermute(low, "mp", [(i, (i + shift) % cores) for i in range(cores)])
        total = total + other.astype(F32)
    return total


def across(values, bit, count):
    return lax.ppermute(values, "dp", [(i, i ^ (1 << bit)) for i in range(count)])


def parted(array, remaining, bit, mine):
    place = sorted(remaining).index(bit)
    groups, rows, columns = array.shape
    low = 1 << place
    view = array.reshape(groups // (2 * low), 2, low, rows, columns)

    def pick(which):
        return lax.dynamic_index_in_dim(view, which, 1, keepdims=False).reshape(
            groups // 2, rows, columns
        )

    return pick(mine), pick(1 - mine)


def halving(first, second, count):
    bits = count.bit_length() - 1
    me = lax.axis_index("dp")
    arrays = [a.reshape(count, a.shape[0] // count, a.shape[1]) for a in (first, second)]
    left = [list(range(bits)), list(range(bits))]
    for order in ((0, 1), (1, 0)):
        for which in (0, 1):
            bit = order[which]
            mine, other = parted(arrays[which], left[which], bit, (me >> bit) & 1)
            got = across(other.astype(BF16), bit, count)
            arrays[which] = mine + got.astype(F32)
            left[which] = [b for b in left[which] if b != bit]
    rest = left[0]
    while rest:
        bit = rest[0]
        halves = [parted(a, rest, bit, (me >> bit) & 1) for a in arrays]
        sent = jnp.concatenate([h[1].astype(BF16) for h in halves], axis=-1)
        got = across(sent, bit, count).astype(F32)
        cut = arrays[0].shape[-1]
        arrays = [halves[0][0] + got[..., :cut], halves[1][0] + got[..., cut:]]
        rest = rest[1:]
    return arrays[0][0], arrays[1][0]


def per_device(
    dp,
    mp,
    tokens,
    cotangent,
    lengths,
    ln1_gain,
    ln1_bias,
    qkv_weight,
    qv_bias,
    out_weight,
    out_bias,
    ln2_gain,
    ln2_bias,
    up_weight,
    up_bias,
    down_weight,
    down_bias,
):
    row_count, width = tokens.shape
    local = qkv_weight.shape[2]
    scale = HEAD_DIM ** (-0.5)
    block = min(256, row_count)
    ends = jnp.cumsum(lengths[0])
    positions = jnp.arange(row_count, dtype=jnp.int32)
    image_ids = jnp.sum((ends[None, :] <= positions[:, None]).astype(jnp.int32), axis=1)
    valid = (image_ids < lengths.shape[1]).astype(F32)
    inputs_f = tokens.astype(F32)
    normed_one, inverse_one = normalize(inputs_f)
    hidden_one = (normed_one * ln1_gain + ln1_bias).astype(BF16)
    planes = jnp.transpose(qkv_weight, (1, 0, 2))

    def project(index):
        return jnp.dot(hidden_one, planes[index], preferred_element_type=F32)

    queries = (project(0) + qv_bias[0]).astype(BF16) * jnp.asarray(scale, BF16)
    keys_all = project(1).astype(BF16)
    values_all = (project(2) + qv_bias[1]).astype(BF16)
    probs, attn_mixed = attention_forward(queries, keys_all, values_all, image_ids, block)
    attn_part = jnp.dot(attn_mixed, out_weight, preferred_element_type=F32)
    after_attn = inputs_f + swap_cores(attn_part, mp) + out_bias
    normed_two, inverse_two = normalize(after_attn)
    hidden_two = (normed_two * ln2_gain + ln2_bias).astype(BF16)
    hidden_pre = jnp.dot(hidden_two, up_weight, preferred_element_type=F32) + up_bias
    activated = jax.nn.gelu(hidden_pre, approximate=True).astype(BF16)
    grad_full = cotangent.astype(F32) * valid[:, None]
    grad_mlp = grad_full.astype(BF16)
    grad_act = jnp.einsum("rd,fd->rf", grad_mlp, down_weight, preferred_element_type=F32)
    grad_pre = gelu_back(hidden_pre, grad_act).astype(BF16)
    norm_part = jnp.einsum("rf,cf->rc", grad_pre, up_weight, preferred_element_type=F32)
    grad_norm = swap_cores(norm_part, mp)
    down_part = jnp.dot(activated, down_weight, preferred_element_type=F32)
    output = (after_attn + swap_cores(down_part, mp) + down_bias).astype(BF16)
    down_grad = jnp.einsum("rd,rf->df", grad_mlp, activated, preferred_element_type=F32)
    up_grad = jnp.einsum("rc,rf->cf", hidden_two, grad_pre, preferred_element_type=F32)
    down_sum, up_sum = halving(down_grad, up_grad, dp)
    down_bias_grad = jnp.sum(grad_mlp.astype(F32), axis=0)
    up_bias_grad = jnp.sum(grad_pre.astype(F32), axis=0)
    ln2_gain_grad = jnp.sum(grad_norm * normed_two, axis=0)
    ln2_bias_grad = jnp.sum(grad_norm, axis=0)
    grad_resid = grad_full + norm_back(grad_norm, normed_two, inverse_two, ln2_gain)
    grad_attn = grad_resid.astype(BF16)
    out_bias_grad = jnp.sum(grad_attn.astype(F32), axis=0)
    out_grad = jnp.einsum("rd,rc->dc", grad_attn, attn_mixed, preferred_element_type=F32)
    grad_mixed = jnp.einsum("rd,cd->rc", grad_attn, out_weight, preferred_element_type=F32)
    grad_proj = attention_backward(
        queries, keys_all, values_all, grad_mixed.astype(BF16), probs, block
    )
    qkv_grad = jnp.einsum("rc,rj->cj", hidden_one, grad_proj, preferred_element_type=F32)
    first_part = sum(
        jnp.einsum(
            "rj,cj->rc",
            grad_proj[:, i * local : (i + 1) * local],
            planes[i],
            preferred_element_type=F32,
        )
        for i in range(3)
    )
    grad_first = swap_cores(first_part, mp)
    cut = (qkv_grad.shape[1] + out_grad.shape[1]) // 2
    left_sum, right_sum = halving(
        qkv_grad[:, :cut], jnp.concatenate([qkv_grad[:, cut:], out_grad], axis=1), dp
    )
    rest = qkv_grad.shape[1] - cut
    qkv_sum = jnp.concatenate([left_sum, right_sum[:, :rest]], axis=1).reshape(-1, 3, local)
    out_sum = right_sum[:, rest:]
    q_bias_grad = jnp.sum(grad_proj[:, :local].astype(F32), axis=0)
    v_bias_grad = jnp.sum(grad_proj[:, 2 * local :].astype(F32), axis=0)
    ln1_gain_grad = jnp.sum(grad_first * normed_one, axis=0)
    ln1_bias_grad = jnp.sum(grad_first, axis=0)
    tokens_grad = grad_resid + norm_back(grad_first, normed_one, inverse_one, ln1_gain)
    small = [
        ln1_gain_grad,
        ln1_bias_grad,
        q_bias_grad,
        v_bias_grad,
        out_bias_grad,
        ln2_gain_grad,
        ln2_bias_grad,
        up_bias_grad,
        down_bias_grad,
    ]
    packed = jnp.concatenate(small).reshape(-1, 128)
    for bit in range(dp.bit_length() - 1):
        packed = packed + across(packed, bit, dp)
    packed = packed.reshape(-1)
    sums = []
    at = 0
    for item in small:
        sums.append(packed[at : at + item.shape[0]])
        at += item.shape[0]
    gain_one, bias_one, q_sum, v_sum, out_bias_sum, gain_two, bias_two, up_bias_sum, down_bias_sum = (
        sums
    )
    return (
        output,
        tokens_grad,
        gain_one,
        bias_one,
        qkv_sum,
        jnp.stack([q_sum, v_sum]),
        out_sum.T,
        out_bias_sum,
        gain_two,
        bias_two,
        up_sum,
        up_bias_sum,
        down_sum.T,
        down_bias_sum,
    )


def solution(mesh):
    return jax.shard_map(
        functools.partial(per_device, mesh.shape["dp"], mesh.shape["mp"]),
        mesh=mesh,
        in_specs=(
            P("dp", None),
            P("dp", None),
            P("dp", None),
            P(),
            P(),
            P(None, None, "mp"),
            P(None, "mp"),
            P("mp", None),
            P(),
            P(),
            P(),
            P(None, "mp"),
            P("mp"),
            P("mp", None),
            P(),
        ),
        out_specs=(
            P("dp", None),
            P("dp", None),
            P(),
            P(),
            P("dp", None, "mp"),
            P(None, "mp"),
            P("mp", "dp"),
            P(),
            P(),
            P(),
            P("dp", "mp"),
            P("mp"),
            P("mp", "dp"),
            P(),
        ),
        check_vma=False,
    )
```
